256 devices in a mesh: space: 64 (over z_lo, x, y), coil: 4 (over z_hi, core).
Axes of the slice: x: 4, y: 4, z: 8 (z_hi: 2, z_lo: 4; z = z_hi * 4 + z_lo), core: 2. Of those that a mesh axis runs over, the one named last changes fastest.
Arguments:
- image: float32 [2, 4, 512, 512], P(None, None, 'space', 'coil'), may hold values from -6 to 6
- maps: float32 [2, 32, 4, 512, 512], P(None, 'coil', None, 'space'), may hold values from -4 to 4
- moment1: float32 [2, 32, 4, 512, 512], P(None, 'coil', None, 'space'), may hold values from -0.75 to 0.75
- moment2: float32 [2, 32, 4, 512, 512], P(None, 'coil', None, 'space'), may hold values from 0.001 to 0.1
- noise: float32 [2, 32, 4, 512, 512], P(None, 'coil', None, 'space'), may hold values from -6 to 6
- kspace: float32 [512, 2, 32, 4, 512], P('space', None, 'coil'), may hold values from -4 to 4
- mask: int32 [512, 512], P('space'), may hold values 0 or 1
Outputs:
- new_maps: float32 [2, 32, 4, 512, 512], P(None, 'coil', None, 'space')
- new_moment1: float32 [2, 32, 4, 512, 512], P(None, 'coil', None, 'space')
- new_moment2: float32 [2, 32, 4, 512, 512], P(None, 'coil', None, 'space')
The draws below stay inside these ranges and needn't reach their ends.
All inputs are finite; a program needn't handle non-finite values. No bound on the sum of `mask` on one device may be relied on, other than what follows from the above.
Results may differ from the reference program's by a relative error of at most 0.00008.
Values sent between devices are 32-bit elements; how exact they have to be, the bound alone decides.
A program may use at most 128 MiB of HBM per device.

```python
import math
import jax
import jax.numpy as jnp
from jax import lax

NY = 512
NZ = 512
COILS = 32
SLICES = 4


def touch_ends(array, rng, least, largest):
    index_at = [jax.random.randint(jax.random.fold_in(rng, axis), (), 0, length) for axis, length in enumerate(array.shape)]
    widest = array.shape.index(max(array.shape))
    neighbour = index_at[:widest] + [(index_at[widest] + 1) % array.shape[widest]] + index_at[widest + 1:]
    return array.at[tuple(index_at)].set(least).at[tuple(neighbour)].set(largest)


def block_scale(stream_key, shape, cuts, low, largest):
    def one(position, blocks):
        steps = jax.random.uniform(jax.random.fold_in(jax.random.fold_in(stream_key, 6), position), (blocks,), jnp.float32, low / len(cuts), largest / len(cuts))
        return jnp.repeat(jnp.exp(steps), shape[position] // blocks).reshape((-1,) + (1,) * (len(shape) - position - 1))

    level = one(*cuts[0])
    for cut in cuts[1:]:
        level = level * one(*cut)
    return level


def gaussian(own_key, dims, spread, bound, pieces=(), kind=jnp.bfloat16):
    values = jax.random.normal(own_key, dims, jnp.float32) * spread
    if len(pieces) > 0:
        values = block_scale(own_key, dims, pieces, -0.22, 0.18) * values
    return jnp.clip(values, min=-bound, max=bound).astype(kind)


def setup_inputs(seed: int = 0) -> dict:
    seeds = jax.random.split(jax.random.key(seed), 8)
    return {
        "image": gaussian(seeds[0], (2, SLICES, NZ, NY), 1.0, 6.0, ((2, 64), (3, 4)), jnp.float32),
        "maps": gaussian(seeds[1], (2, COILS, SLICES, NZ, NY), 0.3, 4.0, ((1, 4), (3, 64)), jnp.float32),
        "moment1": gaussian(seeds[2], (2, COILS, SLICES, NZ, NY), 0.05, 0.75, ((1, 4), (3, 64)), jnp.float32),
        "moment2": jnp.clip(jnp.exp(math.log(0.1) - 4.6051702 * jax.random.uniform(seeds[3], (2, COILS, SLICES, NZ, NY), jnp.float32) ** block_scale(seeds[3], (2, COILS, SLICES, NZ, NY), ((1, 4), (3, 64)), -0.2, 0.2)), 0.001, 0.1),
        "noise": gaussian(seeds[4], (2, COILS, SLICES, NZ, NY), 1.0, 6.0, ((1, 4), (3, 64)), jnp.float32),
        "kspace": gaussian(seeds[5], (NY, 2, COILS, SLICES, NZ), 0.3, 4.0, ((0, 64), (2, 4)), jnp.float32),
        "mask": touch_ends((jax.random.randint(seeds[6], (NY, NZ), 0, 3) < 1).astype(jnp.int32), jax.random.fold_in(seeds[6], 1), 0, 1),
    }


beta_first = 0.9
beta_second = 0.999
adam_steps = 10
learn_rate = 0.2
noise_weight = 0.05
epsilon = 1e-08

def reference(image, maps, moment1, moment2, noise, kspace, mask):
    picture = lax.complex(image[0], image[1])
    sensing = lax.complex(maps[0], maps[1])
    coil_images = sensing * picture[None]
    estimate = jnp.swapaxes(jnp.fft.fftn(coil_images, axes=(2, 3), norm='ortho'), 2, 3)
    measured = jnp.transpose(lax.complex(kspace[:, 0], kspace[:, 1]), (1, 2, 0, 3))
    weight = mask.astype(jnp.float32)
    resid = (estimate - measured) * weight[None, None]
    back = jnp.fft.ifftn(jnp.swapaxes(resid, 2, 3), axes=(2, 3), norm='ortho')
    grad = jnp.conj(picture)[None] * back
    grad_parts = jnp.stack([jnp.real(grad), jnp.imag(grad)])
    new_moment1 = beta_first * moment1 + (1.0 - beta_first) * grad_parts
    new_moment2 = beta_second * moment2 + (1.0 - beta_second) * grad_parts * grad_parts
    first_fix = 1.0 - beta_first ** adam_steps
    second_fix = 1.0 - beta_second ** adam_steps
    update = new_moment1 / first_fix / (jnp.sqrt(new_moment2 / second_fix) + epsilon)
    new_maps = maps - learn_rate * update + noise_weight * noise
    return (new_maps, new_moment1, new_moment2)
```

```python
import functools
import math

import jax
import jax.numpy as jnp
import numpy as np
from jax import lax
from jax.experimental import pallas as pl
from jax.experimental.pallas import tpu as pltpu
from jax.sharding import PartitionSpec as P

beta_first = 0.9
beta_second = 0.999
adam_steps = 10
learn_rate = 0.2
noise_weight = 0.05
epsilon = 1e-08

GROUP = 64
CHUNKS = 4
PER = 4 // CHUNKS
ROWS = 8 * PER
MESH = pl.DeviceIdType.MESH
F32 = jnp.float32
BF16 = jnp.bfloat16


def split_table(table):
    table = table.astype(np.float32)
    high = table.astype(jnp.bfloat16)
    low = (table - high.astype(np.float32)).astype(jnp.bfloat16)
    return high, low


@functools.cache
def tables():
    n = np.arange(256)
    angle = 2.0 * math.pi * ((n[:, None] * n[None, :]) % 256) / 256.0
    cos = np.cos(angle) / math.sqrt(512.0)
    sin = np.sin(angle) / math.sqrt(512.0)
    forward = np.stack([np.stack([cos, sin]), np.stack([-sin, cos])])
    t1 = forward.reshape(2, 2, 64, 4, 256).transpose(3, 0, 2, 1, 4).reshape(512, 512)
    t2 = forward.reshape(2, 2, 256, 64, 4).transpose(0, 2, 3, 4, 1).reshape(512, 512)
    t3 = t2.T.copy()
    turn = 2.0 * math.pi * n / 512.0
    upper = (np.arange(128) >= 64)[None, :]
    twist_a = np.where(upper, np.cos(turn)[:, None], 1.0).astype(np.float32)
    twist_b = np.where(upper, np.sin(turn)[:, None], 0.0).astype(np.float32)
    turns = np.stack([np.cos(turn), np.sin(turn)]).astype(np.float32)
    turns = np.concatenate([turns, np.zeros((6, 256), np.float32)])
    return (*split_table(t1), *split_table(t2), *split_table(t3), twist_a, twist_b, turns)


def halves(value):
    high = value.astype(BF16)
    return high, (value - high.astype(F32)).astype(BF16)


def product(left, right, dims=((1,), (0,))):
    (left_high, left_low), (right_high, right_low) = left, right
    dot = functools.partial(lax.dot_general, dimension_numbers=(dims, ((), ())), preferred_element_type=F32)
    return dot(left_high, right_high) + (dot(left_high, right_low) + dot(left_low, right_high))


def kernel(
    image, maps, moment1, moment2, noise, kspace, mask, t1h, t1l, t2h, t2l, t3h, t3l, twa, twb, turns,
    out_maps, out_moment1, out_moment2,
    image_v, maps_v, moment1_v, moment2_v, noise_v, kspace_v, t1h_v, t1l_v, t2h_v, t2l_v, t3h_v, t3l_v,
    mixed, stack_v, target, weight, send1, recv1, send2, recv2, total, back,
    load_sem, image_send, image_recv, send_sem1, recv_sem1, send_sem2, recv_sem2, store_sem,
):
    me = lax.axis_index("space")
    coil = lax.axis_index("coil")

    loads = {}
    for index, (name, source, place) in enumerate([
        ("kspace", kspace, kspace_v), ("maps", maps, maps_v), ("t1h", t1h, t1h_v), ("t1l", t1l, t1l_v),
        ("t2h", t2h, t2h_v), ("t2l", t2l, t2l_v), ("t3h", t3h, t3h_v), ("t3l", t3l, t3l_v),
        ("moment1", moment1, moment1_v), ("moment2", moment2, moment2_v), ("noise", noise, noise_v),
    ]):
        loads[name] = pltpu.make_async_copy(source, place, load_sem.at[index])
        loads[name].start()

    barrier = pltpu.get_barrier_semaphore()
    for step in range(1, 4):
        pl.semaphore_signal(barrier, inc=1, device_id=(me, (coil + step) % 4), device_id_type=MESH)

    def greet(step, carry):
        pl.semaphore_signal(barrier, inc=1, device_id=((me + step) % GROUP, coil), device_id_type=MESH)
        return carry

    lax.fori_loop(1, GROUP, greet, 0)

    pl.semaphore_wait(barrier, GROUP + 2)
    own = pltpu.make_async_copy(image, image_v.at[coil], image_recv)
    own.start()
    for step in range(1, 4):
        pltpu.make_async_remote_copy(
            image, image_v.at[coil], image_send, image_recv,
            device_id=(me, (coil + step) % 4), device_id_type=MESH,
        ).start()

    loads["kspace"].wait()

    def arrange(pair, carry):
        chunk, part = pair // 2, pair % 2
        for k2 in range(2):
            for c in range(8):
                lines = kspace_v[2 * chunk + k2, part, c]
                for khi in range(2):
                    first = khi * 64 + k2 * 32 + c * 4
                    stack_v[first:first + 4, :] = lines[:, khi * 256:(khi + 1) * 256]
        target[chunk, part] = stack_v[...].T
        return carry

    lax.fori_loop(0, 8, arrange, 0)
    for chunk in range(4):
        lines = mask[2 * chunk:2 * chunk + 2, :].astype(F32)
        blocks = [
            jnp.broadcast_to(lines[k2:k2 + 1, khi * 256:(khi + 1) * 256], (32, 256))
            for khi in range(2) for k2 in range(2)
        ]
        weight[chunk] = jnp.concatenate(blocks, axis=0).T

    loads["maps"].wait()
    pltpu.make_async_copy(image_v, image_v, image_recv).wait()

    def coil_image(c, carry):
        for yh in range(2):
            values = []
            for half in range(2):
                yq = 2 * half + yh
                lanes = slice(yq * 128, (yq + 1) * 128)
                image_real, image_imag = image_v[yq, 0:32, :], image_v[yq, 32:64, :]
                map_real = maps_v[pl.ds(pl.multiple_of(c * 32, 32), 32), lanes]
                map_imag = maps_v[pl.ds(pl.multiple_of(256 + c * 32, 32), 32), lanes]
                values.append(map_real * image_real - map_imag * image_imag)
                values.append(map_real * image_imag + map_imag * image_real)
            cos, sin = turns[0:1, yh * 128:(yh + 1) * 128], turns[1:2, yh * 128:(yh + 1) * 128]
            diff_real, diff_imag = values[0] - values[2], values[1] - values[3]
            real_rows = pl.ds(pl.multiple_of(c * 32, 32), 32)
            imag_rows = pl.ds(pl.multiple_of(256 + c * 32, 32), 32)
            mixed[0, yh, real_rows, :] = values[0] + values[2]
            mixed[0, yh, imag_rows, :] = values[1] + values[3]
            mixed[1, yh, real_rows, :] = diff_real * cos + diff_imag * sin
            mixed[1, yh, imag_rows, :] = diff_imag * cos - diff_real * sin
        return carry

    lax.fori_loop(0, 8, coil_image, 0)

    loads["t1h"].wait()
    loads["t1l"].wait()
    for pair in range(2):
        lines = []
        for zq in (2 * pair, 2 * pair + 1):
            for zp in range(2):
                for k2 in range(2):
                    lines.append(jnp.concatenate([
                        mixed[k2, yh, pl.ds(part * 256 + 2 * zq + zp, 32, stride=8), :]
                        for part in range(2) for yh in range(2)
                    ], axis=1))
        lines = jnp.concatenate(lines, axis=0)
        spectra = product((t1h_v[...], t1l_v[...]), halves(lines), ((1,), (1,)))
        for which in range(2):
            zq = 2 * pair + which
            for j in range(4):
                for part in range(2):
                    first = (j * 2 + part) * 64
                    send1[j // PER, pl.ds((j % PER) * 8 + zq * 2 + part, 64, stride=ROWS), :] = (
                        spectra[first:first + 64, which * 128:(which + 1) * 128]
                    )

    z_at, x_at, y_at = me // 16, me // 4 % 4, me % 4
    mine = pl.ds(pl.multiple_of(me * ROWS, ROWS), ROWS)

    def exchange(chunk, source, place, send_sem, recv_sem):
        pltpu.make_async_copy(source.at[chunk, mine], place.at[chunk, mine], recv_sem.at[chunk]).start()
        for dz in (2, 1, 3, 0):

            def send(step, carry):
                other = (z_at + dz) % 4 * 16 + (x_at + step // 4) % 4 * 4 + (y_at + step) % 4
                theirs = pl.ds(pl.multiple_of(other * ROWS, ROWS), ROWS)
                pltpu.make_async_remote_copy(
                    source.at[chunk, theirs], place.at[chunk, mine], send_sem.at[chunk], recv_sem.at[chunk],
                    device_id=(other, coil), device_id_type=MESH,
                ).start()
                return carry

            lax.fori_loop(1 if dz == 0 else 0, 16, send, 0)

    def arrived(chunk, place, recv_sem):
        pltpu.make_async_copy(place.at[chunk], place.at[chunk], recv_sem.at[chunk]).wait()

    def sent(chunk, source, send_sem):
        whole = source.at[chunk, pl.ds(0, (GROUP - 1) * ROWS)]
        pltpu.make_async_copy(whole, whole, send_sem.at[chunk]).wait()

    for chunk in range(CHUNKS):
        exchange(chunk, send1, recv1, send_sem1, recv_sem1)

    for name in ("t2h", "t2l", "t3h", "t3l"):
        loads[name].wait()
    upper = lax.broadcasted_iota(jnp.int32, (256, 128), 1) >= 64
    sign = jnp.where(upper, -1.0, 1.0).astype(F32)

    for chunk in range(CHUNKS):
        arrived(chunk, recv1, recv_sem1)
        for within in range(PER):
            j = chunk * PER + within
            if PER == 1:
                slabs = recv1[chunk]
            else:
                slabs = recv1[chunk].reshape(GROUP, ROWS, 128)[:, within * 8:within * 8 + 8].reshape(512, 128)
            lines = product((t2h_v[...], t2l_v[...]), halves(slabs))
            real, imag = lines[:256], lines[256:]
            turn_a, turn_b = twa[...], twb[...]
            real, imag = turn_a * real + turn_b * imag, turn_a * imag - turn_b * real
            real = pltpu.roll(real, 64, 1) + sign * real
            imag = pltpu.roll(imag, 64, 1) + sign * imag
            real = (real - target[j, 0]) * weight[j]
            imag = (imag - target[j, 1]) * weight[j]
            real = pltpu.roll(real, 64, 1) + sign * real
            imag = pltpu.roll(imag, 64, 1) + sign * imag
            real, imag = turn_a * real - turn_b * imag, turn_a * imag + turn_b * real
            lines = jnp.concatenate([real, imag], axis=0)
            slabs = product((t3h_v[...], t3l_v[...]), halves(lines))
            if PER == 1:
                send2[chunk] = slabs
            else:
                for d in range(GROUP):
                    send2[chunk, d * ROWS + within * 8:d * ROWS + within * 8 + 8, :] = slabs[d * 8:d * 8 + 8]
        exchange(chunk, send2, recv2, send_sem2, recv_sem2)

    for chunk in range(CHUNKS):
        arrived(chunk, recv2, recv_sem2)
        for within in range(PER):
            j = chunk * PER + within
            columns = jnp.concatenate([
                jnp.concatenate([
                    recv2[chunk, pl.ds(within * 8 + zq * 2 + part, 64, stride=ROWS), :] for part in range(2)
                ], axis=0).T
                for zq in range(4)
            ], axis=0)
            part_sum = product(halves(columns), (t1h_v[j * 128:(j + 1) * 128, :], t1l_v[j * 128:(j + 1) * 128, :]))
            total[...] = part_sum if j == 0 else total[...] + part_sum

    for name in ("moment1", "moment2", "noise"):
        loads[name].wait()
    for zq in range(4):
        for zp in range(2):
            even = total[zq * 128 + zp * 64:zq * 128 + zp * 64 + 32, :]
            odd = total[zq * 128 + zp * 64 + 32:zq * 128 + zp * 64 + 64, :]
            cos, sin = turns[0:1, :], turns[1:2, :]
            odd_real = cos * odd[:, :256] - sin * odd[:, 256:]
            odd_imag = cos * odd[:, 256:] + sin * odd[:, :256]
            for part, (first, second) in enumerate([(even[:, :256], odd_real), (even[:, 256:], odd_imag)]):
                for half, value in enumerate([first + second, first - second]):
                    for yh in range(2):
                        back[part, 2 * half + yh, pl.ds(2 * zq + zp, 32, stride=8), :] = (
                            value[:, yh * 128:(yh + 1) * 128]
                        )

    first_fix = 1.0 / (1.0 - beta_first**adam_steps)
    second_fix = 1.0 / (1.0 - beta_second**adam_steps)

    def finish(c, carry):
        real_rows = pl.ds(pl.multiple_of(c * 32, 32), 32)
        imag_rows = pl.ds(pl.multiple_of(256 + c * 32, 32), 32)
        for yq in range(4):
            lanes = slice(yq * 128, (yq + 1) * 128)
            image_real, image_imag = image_v[yq, 0:32, :], image_v[yq, 32:64, :]
            back_real, back_imag = back[0, yq, real_rows, :], back[1, yq, real_rows, :]
            grads = (
                (real_rows, image_real * back_real + image_imag * back_imag),
                (imag_rows, image_real * back_imag - image_imag * back_real),
            )
            for rows, grad in grads:
                first = beta_first * moment1_v[rows, lanes] + (1.0 - beta_first) * grad
                second = beta_second * moment2_v[rows, lanes] + (1.0 - beta_second) * grad * grad
                update = (first * first_fix) / (jnp.sqrt(second * second_fix) + epsilon)
                moment1_v[rows, lanes] = first
                moment2_v[rows, lanes] = second
                maps_v[rows, lanes] = maps_v[rows, lanes] - learn_rate * update + noise_weight * noise_v[rows, lanes]
        for rows in (real_rows, imag_rows):
            for index, (source, place) in enumerate([
                (maps_v, out_maps), (moment1_v, out_moment1), (moment2_v, out_moment2),
            ]):
                pltpu.make_async_copy(source.at[rows, :], place.at[rows, :], store_sem.at[index]).start()
        return carry

    lax.fori_loop(0, 8, finish, 0)
    whole_image = image_v.at[pl.ds(0, 3)]
    pltpu.make_async_copy(whole_image, whole_image, image_send).wait()
    for chunk in range(CHUNKS):
        sent(chunk, send1, send_sem1)
        sent(chunk, send2, send_sem2)
    for index, (source, place) in enumerate([(maps_v, out_maps), (moment1_v, out_moment1), (moment2_v, out_moment2)]):
        pltpu.make_async_copy(source, place, store_sem.at[index]).wait()


def body(image, maps, moment1, moment2, noise, kspace, mask):
    shape = maps.shape
    rows = [array.reshape(512, 512) for array in (maps, moment1, moment2, noise)]
    constants = [jnp.asarray(table) for table in tables()]
    hbm, vmem = pl.BlockSpec(memory_space=pl.ANY), pl.BlockSpec(memory_space=pltpu.VMEM)
    results = pl.pallas_call(
        kernel,
        out_shape=[jax.ShapeDtypeStruct((512, 512), F32)] * 3,
        in_specs=[hbm] * 6 + [vmem] + [hbm] * 6 + [vmem] * 3,
        out_specs=[hbm] * 3,
        scratch_shapes=[
            pltpu.VMEM((4, 64, 128), F32),
            pltpu.VMEM((512, 512), F32),
            pltpu.VMEM((512, 512), F32),
            pltpu.VMEM((512, 512), F32),
            pltpu.VMEM((512, 512), F32),
            pltpu.VMEM((8, 2, 8, 4, 512), F32),
        ] + [pltpu.VMEM((512, 512), BF16)] * 6 + [
            pltpu.VMEM((2, 2, 512, 128), F32),
            pltpu.VMEM((128, 256), F32),
            pltpu.VMEM((4, 2, 256, 128), F32),
            pltpu.VMEM((4, 256, 128), F32),
        ] + [pltpu.VMEM((CHUNKS, GROUP * ROWS, 128), F32)] * 4 + [
            pltpu.VMEM((512, 512), F32),
            pltpu.VMEM((2, 4, 256, 128), F32),
            pltpu.SemaphoreType.DMA((11,)),
            pltpu.SemaphoreType.DMA,
            pltpu.SemaphoreType.DMA,
            pltpu.SemaphoreType.DMA((CHUNKS,)),
            pltpu.SemaphoreType.DMA((CHUNKS,)),
            pltpu.SemaphoreType.DMA((CHUNKS,)),
            pltpu.SemaphoreType.DMA((CHUNKS,)),
            pltpu.SemaphoreType.DMA((3,)),
        ],
        compiler_params=pltpu.CompilerParams(collective_id=0, has_side_effects=True),
    )(image.reshape(64, 128), *rows, kspace, mask, *constants)
    return tuple(result.reshape(shape) for result in results)


def solution(mesh):
    in_specs = (
        P(None, None, "space", "coil"),
        P(None, "coil", None, "space", None),
        P(None, "coil", None, "space", None),
        P(None, "coil", None, "space", None),
        P(None, "coil", None, "space", None),
        P("space", None, "coil", None, None),
        P("space", None),
    )
    out_specs = (
        P(None, "coil", None, "space", None),
        P(None, "coil", None, "space", None),
        P(None, "coil", None, "space", None),
    )
    return jax.shard_map(body, mesh=mesh, in_specs=in_specs, out_specs=out_specs, check_vma=False)
```
